32 devices in a mesh: dp: 32 (over z, y, x, core).
Axes of the slice: x: 2, y: 2, z: 4, core: 2. Of those that a mesh axis runs over, the one named last changes fastest.
Arguments:
- layer_input: bfloat16 [4096, 768], P('dp'), may hold values from -6 to 6
- encoder_states: bfloat16 [2048, 768], P('dp'), may hold values from -6 to 6
- output_grad: bfloat16 [4096, 768], P('dp'), may hold values from -6 to 6
- self_query: bfloat16 [768, 768], P('dp'), may hold values from -0.078125 to 0.078125
- self_key: bfloat16 [768, 768], P('dp'), may hold values from -0.21875 to 0.21875
- self_value: bfloat16 [768, 768], P('dp'), may hold values from -0.21875 to 0.21875
- self_output: bfloat16 [768, 768], P('dp'), may hold values from -0.625 to 0.625
- cross_query: bfloat16 [768, 768], P('dp'), may hold values from -0.078125 to 0.078125
- cross_key: bfloat16 [768, 768], P('dp'), may hold values from -0.21875 to 0.21875
- cross_value: bfloat16 [768, 768], P('dp'), may hold values from -0.21875 to 0.21875
- cross_output: bfloat16 [768, 768], P('dp'), may hold values from -0.625 to 0.625
- feed_gate: bfloat16 [768, 2048], P('dp'), may hold values from -0.21875 to 0.21875
- feed_up: bfloat16 [768, 2048], P('dp'), may hold values from -0.21875 to 0.21875
- feed_down: bfloat16 [2048, 768], P('dp'), may hold values from -0.125 to 0.125
- gain_self: bfloat16 [768], P('dp'), may hold values from 0.5 to 1.5
- gain_cross: bfloat16 [768], P('dp'), may hold values from 0.5 to 1.5
- gain_feed: bfloat16 [768], P('dp'), may hold values from 0.5 to 1.5
- bias_table: float32 [32, 12], replicated, may hold values from -4 to 4
- target_lengths: int32 [32, 4], P('dp'), may hold values from 1 to 80, 128 in all within a row
- source_lengths: int32 [32, 4], P('dp'), may hold values from 1 to 32, 64 in all within a row
- distance_bucket: int32 [80], replicated, may hold values from 0 to 31
Outputs:
- layer_output: bfloat16 [4096, 768], P('dp')
- input_grad: float32 [4096, 768], P('dp')
- encoder_grad: float32 [2048, 768], P('dp')
- grad_self_query: float32 [768, 768], P('dp')
- grad_self_key: float32 [768, 768], P('dp')
- grad_self_value: float32 [768, 768], P('dp')
- grad_self_output: float32 [768, 768], P('dp')
- grad_cross_query: float32 [768, 768], P('dp')
- grad_cross_key: float32 [768, 768], P('dp')
- grad_cross_value: float32 [768, 768], P('dp')
- grad_cross_output: float32 [768, 768], P('dp')
- grad_feed_gate: float32 [768, 2048], P('dp')
- grad_feed_up: float32 [768, 2048], P('dp')
- grad_feed_down: float32 [2048, 768], P('dp')
- grad_gain_self: float32 [768], P('dp')
- grad_gain_cross: float32 [768], P('dp')
- grad_gain_feed: float32 [768], P('dp')
- grad_bias_table: float32 [32, 12], replicated
The draws below stay inside these ranges and needn't reach their ends.
Inputs may be any that keep to these rules, and one draw needn't show every extreme that they name: `target_lengths`: each row lists the lengths of the 4 decoder sequences of one device in the order of its rows and sums to 128. `source_lengths`: each row lists the lengths of the encoder sequences of the same 4 sequences and sums to 64.
All inputs are finite; a program needn't handle non-finite values.
Results may differ from the reference program's by a relative error of at most 0.03.
The reference program's roundings to bfloat16 on the way count: a program that leaves them out, or rounds other values in their place, can miss the bound.
Values may be sent and summed in bfloat16 or wider, within the bound.
No kernel may reach another device: no remote copies, remote signals or barrier semaphores. Data moves between devices by JAX's collectives and lax.ppermute only.
A program may use at most 192 MiB of HBM per device.

```python
import math
import jax
import jax.numpy as jnp
import numpy as np
from jax import lax

D = 768
H = 12
FF = 2048
NB = 32
TOK_DEV = 128
ENC_DEV = 64
SEQS = 4
SEQ_MAX = 80
ENC_MAX = 32
TOKENS = 4096
ENC_TOKENS = 2048
N_DP = 32


def set_ends(entries, stream_key, least, largest):
    longest = entries.shape.index(max(entries.shape))
    spots = []
    for shift in (0, 1):
        where = [jax.random.randint(jax.random.fold_in(stream_key, axis), (), 0, length) for axis, length in enumerate(entries.shape)]
        where[longest] = (where[longest] + shift) % entries.shape[longest]
        spots.append(tuple(where))
    return entries.at[spots[0]].set(least).at[spots[1]].set(largest)


def block_scale(stream_key, shape, pieces, least, largest):
    def one(dim, shards_of):
        steps = jax.random.uniform(jax.random.fold_in(jax.random.fold_in(stream_key, 6), dim), (shards_of,), jnp.float32, least / len(pieces), largest / len(pieces))
        return jnp.repeat(jnp.exp(steps), shape[dim] // shards_of).reshape((-1,) + (1,) * (len(shape) - dim - 1))

    gain = one(*pieces[0])
    for cut in pieces[1:]:
        gain = gain * one(*cut)
    return gain


def split_up(amount, total, reach, lean):
    weights = [(1 << 20) // math.isqrt(grade ** lean) + 1 for grade in range(2, amount + 1)]
    rest, holding = total - reach - (amount - 1), [1] * (amount - 1)
    while rest > 0:
        candidates = [i for i in range(amount - 1) if holding[i] < reach]
        pool, remaining = sum([weights[i] for i in candidates]), rest
        for i in candidates:
            addition = min(reach - holding[i], max(1, remaining * weights[i] // pool), rest)
            holding[i] = holding[i] + addition
            rest = rest - addition
    return np.array([reach] + holding)


def ragged(own_key, count, total, limit, slope):
    if count == 2:
        one = jax.random.randint(own_key, (), max(1, total - limit), min(limit, total - 1) + 1)
        return jnp.stack([one, total - one])
    sizes = jnp.asarray(split_up(count, total, limit, slope), jnp.int32)
    twos = (count - 1) // 2
    giver, taker = sizes[1:1 + 2 * twos:2], sizes[2:2 + 2 * twos:2]
    room = jnp.minimum(giver - 1, limit - taker)
    passed = jax.random.randint(jax.random.fold_in(own_key, 1), (twos,), 0, 1 << 20) % (room + 1)
    sizes = sizes.at[1:1 + 2 * twos:2].set(giver - passed).at[2:2 + 2 * twos:2].set(taker + passed)
    return sizes[jax.random.permutation(jax.random.fold_in(own_key, 2), count)]


def noise(stream_key, shape, spread, limit, pieces=(), held_as=jnp.bfloat16):
    drawn = spread * jax.random.normal(stream_key, shape, jnp.float32)
    if pieces:
        drawn = drawn * block_scale(stream_key, shape, pieces, -0.22, 0.18)
    return jnp.clip(drawn, -limit, limit).astype(held_as)


def setup_inputs(seed: int = 0) -> dict:
    key_of = jax.random.split(jax.random.key(seed), 22)
    return {
        "layer_input": noise(key_of[0], (TOKENS, D), 1.0, 6.0, ((0, 32),)),
        "encoder_states": noise(key_of[1], (ENC_TOKENS, D), 1.0, 6.0, ((0, 32),)),
        "output_grad": noise(key_of[2], (TOKENS, D), 1.0, 6.0, ((0, 32),)),
        "self_query": noise(key_of[3], (D, D), (8 * D) ** -0.5, 0.078125, ((0, 32),)),
        "self_key": noise(key_of[4], (D, D), D ** -0.5, 0.21875, ((0, 32),)),
        "self_value": noise(key_of[5], (D, D), D ** -0.5, 0.21875, ((0, 32),)),
        "self_output": noise(key_of[6], (D, D), (D // 8) ** -0.5, 0.625, ((0, 32),)),
        "cross_query": noise(key_of[7], (D, D), (8 * D) ** -0.5, 0.078125, ((0, 32),)),
        "cross_key": noise(key_of[8], (D, D), D ** -0.5, 0.21875, ((0, 32),)),
        "cross_value": noise(key_of[9], (D, D), D ** -0.5, 0.21875, ((0, 32),)),
        "cross_output": noise(key_of[10], (D, D), (D // 8) ** -0.5, 0.625, ((0, 32),)),
        "feed_gate": noise(key_of[11], (D, FF), D ** -0.5, 0.21875, ((0, 32),)),
        "feed_up": noise(key_of[12], (D, FF), D ** -0.5, 0.21875, ((0, 32),)),
        "feed_down": noise(key_of[13], (FF, D), FF ** -0.5, 0.125, ((0, 32),)),
        "gain_self": jnp.clip(1.0 + 0.1 * jax.random.normal(key_of[14], (D,), jnp.float32), 0.5, 1.5).astype(jnp.bfloat16),
        "gain_cross": jnp.clip(1.0 + 0.1 * jax.random.normal(key_of[15], (D,), jnp.float32), 0.5, 1.5).astype(jnp.bfloat16),
        "gain_feed": jnp.clip(1.0 + 0.1 * jax.random.normal(key_of[16], (D,), jnp.float32), 0.5, 1.5).astype(jnp.bfloat16),
        "bias_table": noise(key_of[17], (NB, H), 1.0, 4.0, (), jnp.float32),
        "target_lengths": jax.vmap(lambda own: ragged(own, SEQS, TOK_DEV, SEQ_MAX, 2))(jax.random.split(key_of[18], N_DP)).reshape((N_DP, SEQS)).astype(jnp.int32),
        "source_lengths": jax.vmap(lambda own: ragged(own, SEQS, ENC_DEV, ENC_MAX, 2))(jax.random.split(key_of[19], N_DP)).reshape((N_DP, SEQS)).astype(jnp.int32),
        "distance_bucket": set_ends(jax.random.randint(key_of[20], (SEQ_MAX,), 0, NB), jax.random.fold_in(key_of[20], 1), 0, NB - 1).astype(jnp.int32),
    }


EPSILON = 1e-06
MASKED = -1e+30

def matmul(left, right):
    return jnp.dot(left, right, preferred_element_type=jnp.float32)

def rms_norm(hidden, gain_row):
    norm_scale = lax.rsqrt(lax.optimization_barrier(jnp.mean(hidden * hidden, axis=-1, keepdims=True)) + EPSILON)
    return hidden * norm_scale * gain_row

def gated_gelu(gate_part, linear_part):
    return jax.nn.gelu(gate_part, approximate=True) * linear_part

def toeplitz(vector):
    length = vector.shape[0]
    padded = jnp.concatenate([vector[::-1], jnp.zeros((length,), vector.dtype)])
    flattened = jnp.tile(padded, length + 1)[length - 1:length - 1 + length * (2 * length - 1)]
    return flattened.reshape(length, 2 * length - 1)[:, :length]

def segment_ids(lengths, row_total):
    boundary = jnp.cumsum(lengths).astype(jnp.int32)
    row_index = jnp.arange(row_total, dtype=jnp.int32)
    return lax.optimization_barrier(jnp.sum((row_index[:, None] >= boundary[None, :]).astype(jnp.int32), axis=1))

def heads_first(matrix):
    return matrix.reshape(matrix.shape[0], H, -1).transpose(1, 0, 2)

def heads_last(tensor):
    return tensor.transpose(1, 0, 2).reshape(tensor.shape[1], -1)

def head_scores(query_head, key_head, bias_block, allowed):
    scores = matmul(query_head, key_head.T)
    if bias_block is not None:
        scores = scores + bias_block
    return jnp.where(allowed, scores, MASKED)

def head_forward(query_head, key_head, value_head, bias_block, allowed):
    scores = head_scores(query_head, key_head, bias_block, allowed)
    highest = lax.optimization_barrier(jnp.max(scores, axis=1, keepdims=True))
    exp_total = lax.optimization_barrier(jnp.sum(jnp.exp(scores - highest), axis=1, keepdims=True))
    log_total = highest + jnp.log(exp_total)
    weights = jnp.exp(scores - log_total).astype(jnp.bfloat16)
    mixed_rows = matmul(weights, value_head).astype(jnp.bfloat16)
    return (mixed_rows, log_total[:, 0])

def head_backward(query_head, key_head, value_head, mixed_head, grad_head, log_total, bias_block, allowed):
    scores = head_scores(query_head, key_head, bias_block, allowed)
    weights = jnp.where(allowed, jnp.exp(scores - log_total[:, None]), 0.0)
    low_weights = weights.astype(jnp.bfloat16)
    grad_weights = matmul(grad_head, value_head.T)
    row_dot = lax.optimization_barrier(jnp.sum(grad_head.astype(jnp.float32) * mixed_head.astype(jnp.float32), axis=1, keepdims=True))
    grad_scores = weights * (grad_weights - row_dot)
    low_scores = grad_scores.astype(jnp.bfloat16)
    grad_query = matmul(low_scores, key_head).astype(jnp.bfloat16)
    grad_key = matmul(low_scores.T, query_head).astype(jnp.bfloat16)
    grad_value = matmul(low_weights.T, grad_head).astype(jnp.bfloat16)
    return (grad_query, grad_key, grad_value, grad_scores)

def self_attention(query_rows, key_rows, value_rows, bias_rows, allowed):

    def one_head(packed):
        query_head, key_head, value_head, bias_head = packed
        return head_forward(query_head, key_head, value_head, toeplitz(bias_head), allowed)
    mixed_heads, log_total = lax.map(one_head, (heads_first(query_rows), heads_first(key_rows), heads_first(value_rows), bias_rows))
    return (heads_last(mixed_heads), log_total)

def cross_attention(query_rows, key_rows, value_rows, allowed):

    def one_head(packed):
        query_head, key_head, value_head = packed
        return head_forward(query_head, key_head, value_head, None, allowed)
    mixed_heads, log_total = lax.map(one_head, (heads_first(query_rows), heads_first(key_rows), heads_first(value_rows)))
    return (heads_last(mixed_heads), log_total)

def self_attention_grad(query_rows, key_rows, value_rows, mixed_rows, grad_rows, log_total, bias_rows, allowed):

    def one_head(packed):
        query_head, key_head, value_head, mixed_head, grad_head, log_head, bias_head = packed
        bias_block, pullback = jax.vjp(toeplitz, bias_head)
        grad_query, grad_key, grad_value, grad_scores = head_backward(query_head, key_head, value_head, mixed_head, grad_head, log_head, bias_block, allowed)
        return (grad_query, grad_key, grad_value, pullback(grad_scores)[0])
    grad_query, grad_key, grad_value, grad_bias = lax.map(one_head, (heads_first(query_rows), heads_first(key_rows), heads_first(value_rows), heads_first(mixed_rows), heads_first(grad_rows), log_total, bias_rows))
    return (heads_last(grad_query), heads_last(grad_key), heads_last(grad_value), grad_bias)

def cross_attention_grad(query_rows, key_rows, value_rows, mixed_rows, grad_rows, log_total, allowed):

    def one_head(packed):
        query_head, key_head, value_head, mixed_head, grad_head, log_head = packed
        grad_query, grad_key, grad_value, grad_scores = head_backward(query_head, key_head, value_head, mixed_head, grad_head, log_head, None, allowed)
        return (grad_query, grad_key, grad_value)
    grad_query, grad_key, grad_value = lax.map(one_head, (heads_first(query_rows), heads_first(key_rows), heads_first(value_rows), heads_first(mixed_rows), heads_first(grad_rows), log_total))
    return (heads_last(grad_query), heads_last(grad_key), heads_last(grad_value))

def bucket_onehot(distance_bucket, buckets):
    return (distance_bucket[:, None] == jnp.arange(buckets, dtype=jnp.int32)[None, :]).astype(jnp.float32)

def distance_bias(onehot, bias_table, row_count):
    per_distance = jnp.dot(onehot, bias_table, precision=lax.Precision.HIGHEST)
    return jnp.pad(per_distance.T, ((0, 0), (0, row_count - per_distance.shape[0])))

def table_grad(onehot, grad_bias_rows):
    return jnp.dot(onehot.T, grad_bias_rows[:, :onehot.shape[0]].T, precision=lax.Precision.HIGHEST)

def layer_forward(layer_input, encoder_states, target_lengths, source_lengths, bias_rows, attention_full, feed_full):
    self_query, self_key, self_value, self_output, cross_query, cross_key, cross_value, cross_output, gain_self, gain_cross, gain_feed = attention_full
    feed_gate, feed_up, feed_down = feed_full
    row_count = layer_input.shape[0]
    target_segment = segment_ids(target_lengths, row_count)
    source_segment = segment_ids(source_lengths, encoder_states.shape[0])
    position = jnp.arange(row_count, dtype=jnp.int32)
    causal = (target_segment[:, None] == target_segment[None, :]) & (position[None, :] <= position[:, None])
    aligned = target_segment[:, None] == source_segment[None, :]
    resid_zero = layer_input.astype(jnp.float32)
    normed_one = rms_norm(resid_zero, gain_self.astype(jnp.float32)).astype(jnp.bfloat16)
    query_rows = matmul(normed_one, self_query).astype(jnp.bfloat16)
    key_rows = matmul(normed_one, self_key).astype(jnp.bfloat16)
    value_rows = matmul(normed_one, self_value).astype(jnp.bfloat16)
    mixed_one, log_one = self_attention(query_rows, key_rows, value_rows, bias_rows, causal)
    resid_one = resid_zero + matmul(mixed_one, self_output)
    normed_two = rms_norm(resid_one, gain_cross.astype(jnp.float32)).astype(jnp.bfloat16)
    cross_rows = matmul(normed_two, cross_query).astype(jnp.bfloat16)
    cross_keys = matmul(encoder_states, cross_key).astype(jnp.bfloat16)
    cross_values = matmul(encoder_states, cross_value).astype(jnp.bfloat16)
    mixed_two, log_two = cross_attention(cross_rows, cross_keys, cross_values, aligned)
    resid_two = resid_one + matmul(mixed_two, cross_output)
    normed_three = rms_norm(resid_two, gain_feed.astype(jnp.float32)).astype(jnp.bfloat16)
    gate_part = matmul(normed_three, feed_gate)
    linear_part = matmul(normed_three, feed_up)
    hidden = gated_gelu(gate_part, linear_part).astype(jnp.bfloat16)
    layer_output = (resid_two + matmul(hidden, feed_down)).astype(jnp.bfloat16)
    saved_state = (causal, aligned, resid_zero, normed_one, query_rows, key_rows, value_rows, mixed_one, log_one, resid_one, normed_two, cross_rows, cross_keys, cross_values, mixed_two, log_two, resid_two, normed_three, gate_part, linear_part, hidden)
    return (layer_output, saved_state)

def feed_backward(saved_state, output_grad, feed_full, gain_feed):
    feed_gate, feed_up, feed_down = feed_full
    resid_two, normed_three, gate_part, linear_part, hidden = saved_state[16:]
    grad_feed_down = matmul(hidden.T, output_grad)
    grad_hidden = matmul(output_grad, feed_down.T)
    unused_value, pullback = jax.vjp(gated_gelu, gate_part, linear_part)
    grad_gate, grad_linear = pullback(grad_hidden)
    grad_gate = grad_gate.astype(jnp.bfloat16)
    grad_linear = grad_linear.astype(jnp.bfloat16)
    grad_feed_gate = matmul(normed_three.T, grad_gate)
    grad_feed_up = matmul(normed_three.T, grad_linear)
    grad_normed = matmul(grad_gate, feed_gate.T) + matmul(grad_linear, feed_up.T)
    unused_norm, norm_pull = jax.vjp(rms_norm, resid_two, gain_feed.astype(jnp.float32))
    grad_resid_part, grad_gain_feed = norm_pull(grad_normed)
    grad_resid_two = output_grad.astype(jnp.float32) + grad_resid_part
    return ((grad_feed_gate, grad_feed_up, grad_feed_down), grad_gain_feed, grad_resid_two)

def attention_backward(saved_state, grad_resid_two, attention_full, encoder_states, bias_rows):
    causal, aligned, resid_zero, normed_one, query_rows, key_rows, value_rows, mixed_one, log_one, resid_one, normed_two, cross_rows, cross_keys, cross_values, mixed_two, log_two = saved_state[:16]
    self_query, self_key, self_value, self_output, cross_query, cross_key, cross_value, cross_output, gain_self, gain_cross, gain_feed = attention_full
    low_two = grad_resid_two.astype(jnp.bfloat16)
    grad_cross_output = matmul(mixed_two.T, low_two)
    grad_mixed_two = matmul(low_two, cross_output.T).astype(jnp.bfloat16)
    grad_cross_rows, grad_cross_keys, grad_cross_values = cross_attention_grad(cross_rows, cross_keys, cross_values, mixed_two, grad_mixed_two, log_two, aligned)
    grad_cross_query = matmul(normed_two.T, grad_cross_rows)
    grad_cross_key = matmul(encoder_states.T, grad_cross_keys)
    grad_cross_value = matmul(encoder_states.T, grad_cross_values)
    encoder_grad = matmul(grad_cross_keys, cross_key.T) + matmul(grad_cross_values, cross_value.T)
    grad_normed_two = matmul(grad_cross_rows, cross_query.T)
    unused_two, pull_two = jax.vjp(rms_norm, resid_one, gain_cross.astype(jnp.float32))
    grad_part_two, grad_gain_cross = pull_two(grad_normed_two)
    grad_resid_one = grad_resid_two + grad_part_two
    low_one = grad_resid_one.astype(jnp.bfloat16)
    grad_self_output = matmul(mixed_one.T, low_one)
    grad_mixed_one = matmul(low_one, self_output.T).astype(jnp.bfloat16)
    grad_query_rows, grad_key_rows, grad_value_rows, grad_bias_rows = self_attention_grad(query_rows, key_rows, value_rows, mixed_one, grad_mixed_one, log_one, bias_rows, causal)
    grad_self_query = matmul(normed_one.T, grad_query_rows)
    grad_self_key = matmul(normed_one.T, grad_key_rows)
    grad_self_value = matmul(normed_one.T, grad_value_rows)
    grad_normed_one = matmul(grad_query_rows, self_query.T) + matmul(grad_key_rows, self_key.T) + matmul(grad_value_rows, self_value.T)
    unused_one, pull_one = jax.vjp(rms_norm, resid_zero, gain_self.astype(jnp.float32))
    grad_part_one, grad_gain_self = pull_one(grad_normed_one)
    input_grad = grad_resid_one + grad_part_one
    matrices = (grad_self_query, grad_self_key, grad_self_value, grad_self_output, grad_cross_query, grad_cross_key, grad_cross_value, grad_cross_output)
    return (matrices, grad_gain_self, grad_gain_cross, grad_bias_rows, input_grad, encoder_grad)

def reference(layer_input, encoder_states, output_grad, self_query, self_key, self_value, self_output, cross_query, cross_key, cross_value, cross_output, feed_gate, feed_up, feed_down, gain_self, gain_cross, gain_feed, bias_table, target_lengths, source_lengths, distance_bucket):
    attention_full = (self_query, self_key, self_value, self_output, cross_query, cross_key, cross_value, cross_output, gain_self, gain_cross, gain_feed)
    feed_full = (feed_gate, feed_up, feed_down)
    onehot = bucket_onehot(distance_bucket, NB)
    bias_rows = distance_bias(onehot, bias_table, TOK_DEV)
    blocks = (layer_input.reshape(N_DP, TOK_DEV, D), encoder_states.reshape(N_DP, ENC_DEV, D), output_grad.reshape(N_DP, TOK_DEV, D), target_lengths, source_lengths)
    start_attention = tuple((jnp.zeros((D, D), jnp.float32) for index in range(8)))
    start_feed = (jnp.zeros((D, FF), jnp.float32), jnp.zeros((D, FF), jnp.float32), jnp.zeros((FF, D), jnp.float32))
    start_gains = tuple((jnp.zeros((D,), jnp.float32) for index in range(3)))
    start_bias = jnp.zeros((H, TOK_DEV), jnp.float32)

    def run_block(totals, block_item):
        tokens_block, encoder_block, grad_block, target_block, source_block = block_item
        attention_sum, feed_sum, gain_sum, bias_sum = totals
        layer_output, saved_state = layer_forward(tokens_block, encoder_block, target_block, source_block, bias_rows, attention_full, feed_full)
        feed_grads, grad_gain_feed, grad_resid_two = feed_backward(saved_state, grad_block, feed_full, gain_feed)
        matrices, grad_gain_self, grad_gain_cross, grad_bias_rows, input_grad, encoder_grad = attention_backward(saved_state, grad_resid_two, attention_full, encoder_block, bias_rows)
        attention_sum = tuple((left + right for left, right in zip(attention_sum, matrices)))
        feed_sum = tuple((left + right for left, right in zip(feed_sum, feed_grads)))
        gain_sum = (gain_sum[0] + grad_gain_self, gain_sum[1] + grad_gain_cross, gain_sum[2] + grad_gain_feed)
        return ((attention_sum, feed_sum, gain_sum, bias_sum + grad_bias_rows), (layer_output, input_grad, encoder_grad))
    totals, stacked = lax.scan(run_block, (start_attention, start_feed, start_gains, start_bias), blocks)
    attention_sum, feed_sum, gain_sum, bias_sum = totals
    layer_output = stacked[0].reshape(TOKENS, D)
    input_grad = stacked[1].reshape(TOKENS, D)
    encoder_grad = stacked[2].reshape(ENC_TOKENS, D)
    grad_table = table_grad(onehot, bias_sum)
    return (layer_output, input_grad, encoder_grad, attention_sum[0], attention_sum[1], attention_sum[2], attention_sum[3], attention_sum[4], attention_sum[5], attention_sum[6], attention_sum[7], feed_sum[0], feed_sum[1], feed_sum[2], gain_sum[0], gain_sum[1], gain_sum[2], grad_table)
```

```python
import jax
import jax.numpy as jnp
from jax import lax
from jax.sharding import PartitionSpec as P

H = 12
AXIS = "dp"
EPSILON = 1e-06
MASKED = -1e30
BF = jnp.bfloat16
F32 = jnp.float32


def matmul(left, right):
    return jnp.dot(left, right, preferred_element_type=F32)


def matmul_nt(left, right):
    return lax.dot_general(left, right, (((1,), (1,)), ((), ())), preferred_element_type=F32)


def matmul_tn(left, right):
    return lax.dot_general(left, right, (((0,), (0,)), ((), ())), preferred_element_type=F32)


def bit_orders(count):
    bits = count.bit_length() - 1
    assert 1 << bits == count
    first = list(range(bits - 1, -1, -1))
    second = [{1: 2, 2: 1}.get(b, b) if bits > 2 else b for b in first]
    return first, second


def partner(count, bit):
    return [(i, i ^ (1 << bit)) for i in range(count)]


def own_bit(bit):
    return (lax.axis_index(AXIS) >> bit) & 1


def gather(piece, order, count):
    rows, columns = piece.shape
    held, done = piece[None], []
    for bit in order:
        other = lax.ppermute(held, AXIS, partner(count, bit))
        low = 1 << sum(1 for b in done if b < bit)
        shape = (held.shape[0] // low, 1, low, rows, columns)
        mine, theirs = held.reshape(shape), other.reshape(shape)
        upper = own_bit(bit) == 1
        held = jnp.concatenate(
            [jnp.where(upper, theirs, mine), jnp.where(upper, mine, theirs)], axis=1
        ).reshape(-1, rows, columns)
        done.append(bit)
    return held.reshape(count * rows, columns)


def scatter_sum(terms, order, count):
    rows, columns = terms.shape[0] // count, terms.shape[1]
    held = terms.astype(BF).reshape(count, rows, columns)
    left = list(range(count.bit_length() - 1))
    for step, bit in enumerate(order):
        low = 1 << sum(1 for b in left if b < bit)
        view = held.reshape(held.shape[0] // (2 * low), 2, low, rows, columns)
        mine = own_bit(bit)
        sent = lax.dynamic_index_in_dim(view, 1 - mine, 1, keepdims=False)
        kept = lax.dynamic_index_in_dim(view, mine, 1, keepdims=False)
        got = lax.ppermute(sent, AXIS, partner(count, bit))
        total = kept.astype(F32) + got.astype(F32)
        held = (total if step == len(order) - 1 else total.astype(BF)).reshape(-1, rows, columns)
        left.remove(bit)
    return held[0]


def total_sum(values, count):
    for bit in range(count.bit_length() - 1):
        values = values + lax.ppermute(values, AXIS, partner(count, bit))
    return values


def norm_scale_of(hidden):
    return lax.rsqrt(jnp.mean(hidden * hidden, axis=-1, keepdims=True) + EPSILON)


def norm_backward(hidden, scale, gain, cotangent):
    weighted = gain * cotangent
    grad_gain = jnp.sum(cotangent * hidden * scale, axis=0)
    inner = jnp.mean(weighted * hidden, axis=-1, keepdims=True)
    return scale * weighted - hidden * (scale * scale * scale) * inner, grad_gain


def toeplitz(vector):
    length = vector.shape[0]
    padded = jnp.concatenate([vector[::-1], jnp.zeros((length,), vector.dtype)])
    flattened = jnp.tile(padded, length + 1)[length - 1 : length - 1 + length * (2 * length - 1)]
    return flattened.reshape(length, 2 * length - 1)[:, :length]


def segment_ids(lengths, row_total):
    boundary = jnp.cumsum(lengths)
    row_index = jnp.arange(row_total, dtype=jnp.int32)
    return jnp.sum((row_index[:, None] >= boundary[None, :]).astype(jnp.int32), axis=1)


def heads_first(matrix):
    return matrix.reshape(matrix.shape[0], H, -1).transpose(1, 0, 2)


def heads_last(tensor):
    return tensor.transpose(1, 0, 2).reshape(tensor.shape[1], -1)


def batched(left, right, left_dim, right_dim):
    return lax.dot_general(
        left, right, (((left_dim,), (right_dim,)), ((0,), (0,))), preferred_element_type=F32
    )


def attend(query, key, value, bias, allowed):
    scores = batched(query, key, 2, 2)
    if bias is not None:
        scores = scores + bias
    scores = jnp.where(allowed[None], scores, MASKED)
    highest = jnp.max(scores, axis=2, keepdims=True)
    log_total = highest + jnp.log(jnp.sum(jnp.exp(scores - highest), axis=2, keepdims=True))
    weights = jnp.where(allowed[None], jnp.exp(scores - log_total), 0.0)
    mixed = batched(weights.astype(BF), value, 2, 1).astype(BF)
    return mixed, weights


def attend_backward(query, key, value, mixed, grad, weights):
    grad_weights = batched(grad, value, 2, 2)
    row_dot = jnp.sum(grad.astype(F32) * mixed.astype(F32), axis=2, keepdims=True)
    grad_scores = weights * (grad_weights - row_dot)
    low = grad_scores.astype(BF)
    grad_query = batched(low, key, 2, 1).astype(BF)
    grad_key = batched(low, query, 1, 1).astype(BF)
    grad_value = batched(weights.astype(BF), grad, 1, 1).astype(BF)
    return grad_query, grad_key, grad_value, grad_scores


def body(
    layer_input, encoder_states, output_grad,
    self_query, self_key, self_value, self_output,
    cross_query, cross_key, cross_value, cross_output,
    feed_gate, feed_up, feed_down,
    gain_self, gain_cross, gain_feed,
    bias_table, target_lengths, source_lengths, distance_bucket, *, count,
):
    order_a, order_b = bit_orders(count)
    width = layer_input.shape[1]
    rows = gain_self.shape[0]
    gains = jnp.stack([gain_self, gain_cross, gain_feed], axis=1)
    gains = jnp.pad(gains, ((0, 0), (0, 128 - gains.shape[1])))
    self_a = gather(jnp.concatenate([self_query, self_key, gains], axis=1), order_a, count)
    self_b = gather(jnp.concatenate([self_value, self_output], axis=1), order_b, count)
    cross_a = gather(jnp.concatenate([cross_key, cross_value], axis=1), order_a, count)
    cross_b = gather(jnp.concatenate([cross_query, cross_output], axis=1), order_b, count)
    gate = gather(feed_gate, order_a, count)
    up = gather(feed_up, order_b, count)
    half = feed_down.shape[1] // 2
    down_a = gather(feed_down[:, :half], order_a, count)
    down_b = gather(feed_down[:, half:], order_b, count)

    row_count = layer_input.shape[0]
    onehot = (
        distance_bucket[:, None] == jnp.arange(bias_table.shape[0], dtype=jnp.int32)[None, :]
    ).astype(F32)
    per_distance = jnp.dot(onehot, bias_table, precision=lax.Precision.HIGHEST)
    bias_rows = jnp.pad(per_distance.T, ((0, 0), (0, row_count - per_distance.shape[0])))
    bias, bias_pull = jax.vjp(jax.vmap(toeplitz), bias_rows)
    target_segment = segment_ids(target_lengths[0], row_count)
    source_segment = segment_ids(source_lengths[0], encoder_states.shape[0])
    position = jnp.arange(row_count, dtype=jnp.int32)
    causal = (target_segment[:, None] == target_segment[None, :]) & (
        position[None, :] <= position[:, None]
    )
    aligned = target_segment[:, None] == source_segment[None, :]

    gain_rows = self_a[:, 2 * width : 2 * width + 3].astype(F32).T
    gain_one, gain_two, gain_three = gain_rows[0:1], gain_rows[1:2], gain_rows[2:3]
    weight_v, weight_o = self_b[:, :width], self_b[:, width:]
    weight_qk = self_a[:, : 2 * width]
    weight_cq, weight_co = cross_b[:, :width], cross_b[:, width:]

    resid_zero = layer_input.astype(F32)
    scale_one = norm_scale_of(resid_zero)
    normed_one = (resid_zero * scale_one * gain_one).astype(BF)
    query_key = matmul(normed_one, weight_qk).astype(BF)
    value_rows = matmul(normed_one, weight_v).astype(BF)
    query_h, key_h = heads_first(query_key[:, :width]), heads_first(query_key[:, width:])
    value_h = heads_first(value_rows)
    mixed_one_h, weights_one = attend(query_h, key_h, value_h, bias, causal)
    mixed_one = heads_last(mixed_one_h)
    resid_one = resid_zero + matmul(mixed_one, weight_o)
    scale_two = norm_scale_of(resid_one)
    normed_two = (resid_one * scale_two * gain_two).astype(BF)
    cross_rows_h = heads_first(matmul(normed_two, weight_cq).astype(BF))
    cross_kv = matmul(encoder_states, cross_a).astype(BF)
    cross_keys_h, cross_values_h = heads_first(cross_kv[:, :width]), heads_first(cross_kv[:, width:])
    mixed_two_h, weights_two = attend(cross_rows_h, cross_keys_h, cross_values_h, None, aligned)
    mixed_two = heads_last(mixed_two_h)
    resid_two = resid_one + matmul(mixed_two, weight_co)
    scale_three = norm_scale_of(resid_two)
    normed_three = (resid_two * scale_three * gain_three).astype(BF)
    gate_part = matmul(normed_three, gate)
    linear_part = matmul(normed_three, up)
    hidden_f32, pullback = jax.vjp(
        lambda g, l: jax.nn.gelu(g, approximate=True) * l, gate_part, linear_part
    )
    hidden = hidden_f32.astype(BF)
    layer_output = jnp.concatenate(
        [
            resid_two[:, :half] + matmul(hidden, down_a),
            resid_two[:, half:] + matmul(hidden, down_b),
        ],
        axis=1,
    ).astype(BF)

    back_a, back_b = order_a[::-1], order_b[::-1]
    share_down_a = scatter_sum(matmul_tn(hidden, output_grad[:, :half]), back_a, count)
    share_down_b = scatter_sum(matmul_tn(hidden, output_grad[:, half:]), back_b, count)
    grad_hidden = matmul_nt(output_grad[:, :half], down_a) + matmul_nt(output_grad[:, half:], down_b)
    grad_gate, grad_linear = pullback(grad_hidden)
    grad_gate, grad_linear = grad_gate.astype(BF), grad_linear.astype(BF)
    share_gate = scatter_sum(matmul_tn(normed_three, grad_gate), back_a, count)
    share_up = scatter_sum(matmul_tn(normed_three, grad_linear), back_b, count)
    grad_normed = matmul_nt(grad_gate, gate) + matmul_nt(grad_linear, up)
    part, grad_gain_feed = norm_backward(resid_two, scale_three, gain_three, grad_normed)
    grad_resid_two = output_grad.astype(F32) + part

    low_two = grad_resid_two.astype(BF)
    share_co = scatter_sum(matmul_tn(mixed_two, low_two), back_a, count)
    grad_mixed_two = heads_first(matmul_nt(low_two, weight_co).astype(BF))
    grad_cq, grad_ck, grad_cv, _ = attend_backward(
        cross_rows_h, cross_keys_h, cross_values_h, mixed_two_h, grad_mixed_two, weights_two
    )
    grad_cross_rows = heads_last(grad_cq)
    grad_cross_kv = jnp.concatenate([heads_last(grad_ck), heads_last(grad_cv)], axis=1)
    share_cq = scatter_sum(matmul_tn(normed_two, grad_cross_rows), back_b, count)
    terms_kv = matmul_tn(encoder_states, grad_cross_kv)
    share_ck = scatter_sum(terms_kv[:, :width], back_a, count)
    share_cv = scatter_sum(terms_kv[:, width:], back_b, count)
    encoder_grad = matmul_nt(grad_cross_kv, cross_a)
    part, grad_gain_cross = norm_backward(
        resid_one, scale_two, gain_two, matmul_nt(grad_cross_rows, weight_cq)
    )
    grad_resid_one = grad_resid_two + part

    low_one = grad_resid_one.astype(BF)
    share_o = scatter_sum(matmul_tn(mixed_one, low_one), back_a, count)
    grad_mixed_one = heads_first(matmul_nt(low_one, weight_o).astype(BF))
    grad_q, grad_k, grad_v, grad_scores = attend_backward(
        query_h, key_h, value_h, mixed_one_h, grad_mixed_one, weights_one
    )
    grad_qk = jnp.concatenate([heads_last(grad_q), heads_last(grad_k)], axis=1)
    grad_value_rows = heads_last(grad_v)
    share_v = scatter_sum(matmul_tn(normed_one, grad_value_rows), back_b, count)
    terms_qk = matmul_tn(normed_one, grad_qk)
    share_q = scatter_sum(terms_qk[:, :width], back_a, count)
    share_k = scatter_sum(terms_qk[:, width:], back_b, count)
    part, grad_gain_self = norm_backward(
        resid_zero, scale_one, gain_one,
        matmul_nt(grad_qk, weight_qk) + matmul_nt(grad_value_rows, weight_v),
    )
    input_grad = grad_resid_one + part
    grad_bias_rows = bias_pull(grad_scores)[0]
    grad_table = jnp.dot(
        onehot.T, grad_bias_rows[:, : onehot.shape[0]].T, precision=lax.Precision.HIGHEST
    )
    table_rows = jnp.pad(grad_table, ((0, 0), (0, width - grad_table.shape[1])))
    small = jnp.concatenate(
        [grad_gain_self[None], grad_gain_cross[None], grad_gain_feed[None], table_rows], axis=0
    )
    small = total_sum(small, count)
    own = lax.dynamic_slice_in_dim(small[:3], lax.axis_index(AXIS) * rows, rows, axis=1)
    return (
        layer_output, input_grad, encoder_grad,
        share_q, share_k, share_v, share_o,
        share_cq, share_ck, share_cv, share_co,
        share_gate, share_up, jnp.concatenate([share_down_a, share_down_b], axis=1),
        own[0], own[1], own[2], small[3:, : grad_table.shape[1]],
    )


def solution(mesh):
    count = mesh.shape[AXIS]
    rows, flat, full = P(AXIS, None), P(AXIS), P()

    def step(*args):
        return body(*args, count=count)

    return jax.shard_map(
        step,
        mesh=mesh,
        in_specs=(rows,) * 14 + (flat,) * 3 + (full, rows, rows, full),
        out_specs=(rows,) * 14 + (flat,) * 3 + (full,),
        check_vma=False,
    )
```

```python
from functools import partial

import jax
import jax.numpy as jnp
from jax import lax
from jax.experimental import pallas as pl
from jax.experimental.pallas import tpu as pltpu
from jax.sharding import PartitionSpec as P

H = 12
AXIS = "dp"
EPSILON = 1e-06
MASKED = -1e30
BF = jnp.bfloat16
F32 = jnp.float32


def matmul(left, right):
    return jnp.dot(left, right, preferred_element_type=F32)


def matmul_nt(left, right):
    return lax.dot_general(left, right, (((1,), (1,)), ((), ())), preferred_element_type=F32)


def matmul_tn(left, right):
    return lax.dot_general(left, right, (((0,), (0,)), ((), ())), preferred_element_type=F32)


def partner(count, bit):
    return [(i, i ^ (1 << bit)) for i in range(count)]


def own_bit(bit):
    return (lax.axis_index(AXIS) >> bit) & 1


def tied(*values):
    return lax.optimization_barrier(values)


def split_bits(count):
    bits = count.bit_length() - 1
    assert 1 << bits == count and bits > 2
    return list(range(bits - 1, 2, -1)), (2, 1), 0


def swap_blocks(held, done, bit, count):
    other = lax.ppermute(held, AXIS, partner(count, bit))
    rows, columns = held.shape[1:]
    low = 1 << sum(1 for b in done if b < bit)
    shape = (held.shape[0] // low, 1, low, rows, columns)
    mine, theirs = held.reshape(shape), other.reshape(shape)
    upper = own_bit(bit) == 1
    return jnp.concatenate(
        [jnp.where(upper, theirs, mine), jnp.where(upper, mine, theirs)], axis=1
    ).reshape(-1, rows, columns)


def gather_high(piece, count):
    high, _, _ = split_bits(count)
    held, done = piece[None], []
    for bit in high:
        held = swap_blocks(held, done, bit, count)
        done.append(bit)
    return held


def gather_middle(held, cut, count):
    high, (left, right), _ = split_bits(count)
    halves = []
    for part, pair in ((held[:, :, :cut], (left, right)), (held[:, :, cut:], (right, left))):
        done = list(high)
        for bit in pair:
            part = swap_blocks(part, done, bit, count)
            done.append(bit)
        halves.append(part)
    return halves


def gather_last(halves, count):
    high, middle, lowest = split_bits(count)
    done = [*high, *middle]
    return [swap_blocks(p, done, lowest, count).reshape(-1, p.shape[2]) for p in halves]


def fold(held, left, bit, count, last=False):
    rows, columns = held.shape[1:]
    low = 1 << sum(1 for b in left if b < bit)
    view = held.reshape(held.shape[0] // (2 * low), 2, low, rows, columns)
    mine = own_bit(bit)
    sent = lax.dynamic_index_in_dim(view, 1 - mine, 1, keepdims=False)
    kept = lax.dynamic_index_in_dim(view, mine, 1, keepdims=False)
    got = lax.ppermute(sent, AXIS, partner(count, bit))
    total = kept.astype(F32) + got.astype(F32)
    return (total if last else total.astype(BF)).reshape(-1, rows, columns)


class Reduction:
    def __init__(self, first, second, count):
        rows = first.shape[0] // count
        self.count, self.step = count, 0
        self.parts = [t.reshape(count, rows, t.shape[1]) for t in (first, second)]
        high, (one, two), lowest = split_bits(count)
        self.high = high[::-1]
        self.orders = ((lowest, one, two), (lowest, two, one))
        self.left = [list(range(count.bit_length() - 1)) for _ in range(2)]

    def advance(self):
        if self.step < 3:
            for side in range(2):
                bit = self.orders[side][self.step]
                self.parts[side] = fold(self.parts[side], self.left[side], bit, self.count)
                self.left[side].remove(bit)
        else:
            if self.step == 3:
                self.parts = [jnp.concatenate(self.parts, axis=2)]
            bit = self.high[self.step - 3]
            last = self.step - 2 == len(self.high)
            self.parts = [fold(self.parts[0], self.left[0], bit, self.count, last)]
            self.left[0].remove(bit)
        self.step += 1

    def tie(self, *values):
        out = tied(*self.parts, *values)
        self.parts = list(out[: len(self.parts)])
        return out[len(self.parts) :]

    def finish(self):
        while self.left[0]:
            self.advance()
        return self.parts[0][0]


def total_sum(values, count):
    for bit in range(count.bit_length() - 1):
        values = values + lax.ppermute(values, AXIS, partner(count, bit))
    return values


def norm_scale_of(hidden):
    return lax.rsqrt(jnp.mean(hidden * hidden, axis=-1, keepdims=True) + EPSILON)


def norm_backward(hidden, gain, cotangent):
    scale = norm_scale_of(hidden)
    weighted = gain * cotangent
    grad_gain = jnp.sum(cotangent * hidden * scale, axis=0, keepdims=True)
    inner = jnp.mean(weighted * hidden, axis=-1, keepdims=True)
    return scale * weighted - hidden * (scale * scale * scale) * inner, grad_gain


def toeplitz(vector):
    length = vector.shape[0]
    padded = jnp.concatenate([vector[::-1], jnp.zeros((length,), vector.dtype)])
    flattened = jnp.tile(padded, length + 1)[length - 1 : length - 1 + length * (2 * length - 1)]
    return flattened.reshape(length, 2 * length - 1)[:, :length]


def segment_ids(lengths, row_total):
    boundary = jnp.cumsum(lengths)
    row_index = jnp.arange(row_total, dtype=jnp.int32)
    return jnp.sum((row_index[:, None] >= boundary[None, :]).astype(jnp.int32), axis=1)


LANES = 128


def pair_stack(block, per_head):
    first = lax.broadcasted_iota(jnp.int32, block.shape, 1) < per_head
    zero = jnp.zeros_like(block)
    return jnp.concatenate([jnp.where(first, block, zero), jnp.where(first, zero, block)], axis=0)


def side_by_side(stacked):
    rows = stacked.shape[0] // 2
    return jnp.concatenate([stacked[:rows], stacked[rows:]], axis=1)


def attention_pair(query, key, value, bias, per_head):
    scores = matmul_nt(pair_stack(query, per_head), key) + bias
    highest = jnp.max(scores, axis=1, keepdims=True)
    total = jnp.sum(jnp.exp(scores - highest), axis=1, keepdims=True)
    weights = jnp.exp(scores - (highest + jnp.log(total)))
    mixed = matmul(side_by_side(weights.astype(BF)), pair_stack(value, per_head)).astype(BF)
    return mixed, weights


def attention_pair_grad(query, key, value, mixed, grad, weights, per_head):
    product = grad.astype(F32) * mixed.astype(F32)
    first = lax.broadcasted_iota(jnp.int32, product.shape, 1) < per_head
    row_dot = jnp.concatenate(
        [
            jnp.sum(jnp.where(first, product, 0.0), axis=1, keepdims=True),
            jnp.sum(jnp.where(first, 0.0, product), axis=1, keepdims=True),
        ],
        axis=0,
    )
    grad_stack = pair_stack(grad, per_head)
    grad_scores = weights * (matmul_nt(grad_stack, value) - row_dot)
    low = grad_scores.astype(BF)
    grad_query = matmul(side_by_side(low), pair_stack(key, per_head)).astype(BF)
    grad_key = matmul_tn(low, pair_stack(query, per_head)).astype(BF)
    grad_value = matmul_tn(weights.astype(BF), grad_stack).astype(BF)
    return grad_query, grad_key, grad_value, grad_scores


SUBLANES = 8


def tile_block(width, inner):
    block = SUBLANES
    while block * inner % (width * SUBLANES):
        block += SUBLANES
    return block


def to_tiles(array, block, inner):
    width = array.shape[1]
    deep = block * inner // width
    tiles = array.reshape(-1, deep // SUBLANES, SUBLANES, width // LANES, LANES)
    tiles = tiles.transpose(0, 1, 3, 2, 4)
    tiles = tiles.reshape(-1, block // SUBLANES, inner // LANES, SUBLANES, LANES)
    return tiles.transpose(0, 1, 3, 2, 4).reshape(-1, inner)


def from_tiles(array, block, width):
    inner = array.shape[1]
    deep = block * inner // width
    tiles = array.reshape(-1, block // SUBLANES, SUBLANES, inner // LANES, LANES)
    tiles = tiles.transpose(0, 1, 3, 2, 4)
    tiles = tiles.reshape(-1, deep // SUBLANES, width // LANES, SUBLANES, LANES)
    return tiles.transpose(0, 1, 3, 2, 4).reshape(-1, width)


def tile_runs(block, width, inner):
    runs, wide, deep = [], width // LANES, inner // LANES
    for tile in range(block // SUBLANES * deep):
        here = (tile // deep, tile // wide)
        if runs and runs[-1][0] == here:
            runs[-1][3] += LANES
        else:
            runs.append([here, tile % deep * LANES, tile % wide * LANES, LANES])
    return [(h[0] * SUBLANES, c, h[1] * SUBLANES, d, n) for h, c, d, n in runs]


def diagonal_sums(block):
    rows, columns = block.shape
    while rows > 1:
        rows //= 2
        block = block[:rows] + pltpu.roll(block[rows:], (columns - rows) % columns, 1)
    return block


def gain_rows_of(columns):
    return columns.astype(F32).T


def self_forward(per_head, x_ref, wa_ref, wb_ref, bias_ref,
                 gains_ref, normed_ref, qkv_ref, mixed_ref, weights_ref, resid_ref):
    width = x_ref.shape[1]
    rows = x_ref.shape[0]
    gains = gain_rows_of(wa_ref[:, 2 * width :])[:8]
    gains_ref[...] = gains
    resid = x_ref[...].astype(F32)
    normed = (resid * norm_scale_of(resid) * gains[0:1]).astype(BF)
    normed_ref[...] = normed
    qkv_ref[:, : 2 * width] = matmul(normed, wa_ref[:, : 2 * width]).astype(BF)
    qkv_ref[:, 2 * width :] = matmul(normed, wb_ref[:, :width]).astype(BF)
    for pair in range(width // (2 * per_head)):
        at = pl.ds(pair * 2 * per_head, 2 * per_head)
        key_at = pl.ds(width + pair * 2 * per_head, 2 * per_head)
        value_at = pl.ds(2 * width + pair * 2 * per_head, 2 * per_head)
        mixed, weights = attention_pair(
            qkv_ref[:, at], qkv_ref[:, key_at], qkv_ref[:, value_at],
            bias_ref[pl.ds(pair * 2 * rows, 2 * rows), :], per_head,
        )
        mixed_ref[:, at] = mixed
        weights_ref[pl.ds(pair * 2 * rows, 2 * rows), :] = weights
    resid_ref[...] = resid + matmul(mixed_ref[...], wb_ref[:, width:])


def cross_forward(per_head, resid_ref, enc_ref, wa_ref, wb_ref, gains_ref, mask_ref,
                  normed_ref, rows_ref, kv_ref, mixed_ref, weights_ref, out_ref, next_ref):
    rows, width = resid_ref.shape
    resid = resid_ref[...]
    normed = (resid * norm_scale_of(resid) * gains_ref[1:2, :]).astype(BF)
    normed_ref[...] = normed
    rows_ref[...] = matmul(normed, wb_ref[:, :width]).astype(BF)
    kv_ref[...] = matmul(enc_ref[...], wa_ref[...]).astype(BF)
    mask = jnp.concatenate([mask_ref[...], mask_ref[...]], axis=0)
    for pair in range(width // (2 * per_head)):
        at = pl.ds(pair * 2 * per_head, 2 * per_head)
        value_at = pl.ds(width + pair * 2 * per_head, 2 * per_head)
        mixed, weights = attention_pair(
            rows_ref[:, at], kv_ref[:, at], kv_ref[:, value_at], mask, per_head
        )
        mixed_ref[:, at] = mixed
        weights_ref[pl.ds(pair * 2 * rows, 2 * rows), :] = weights
    resid = resid + matmul(mixed_ref[...], wb_ref[:, width:])
    out_ref[...] = resid
    next_ref[...] = (resid * norm_scale_of(resid) * gains_ref[2:3, :]).astype(BF)


def feed_step(chunk, block, resid_ref, normed_ref, grad_ref, gains_ref, feed_ref,
              out_ref, grad_resid_ref, grad_gain_ref, terms_ref,
              weights, down, terms, terms_down, in_sem, down_sem, out_sem, down_out_sem):
    width = resid_ref.shape[1]
    inner = down.shape[0]
    steps = inner // chunk
    deep = block * inner // width
    runs = tile_runs(block, width, inner)

    def columns(step, side):
        return pl.ds(side * inner + step * chunk, chunk)

    def load(step, side):
        at = columns(step, side)
        return pltpu.make_async_copy(feed_ref.at[:, at], weights.at[:, at], in_sem.at[step, side])

    def save(step, side):
        at = columns(step, side)
        return pltpu.make_async_copy(terms.at[:, at], terms_ref.at[:, at], out_sem.at[step, side])

    def tile_copies(group, sides, hbm, vmem, sem):
        for row, column, to_row, to_column, length in runs:
            far = hbm.at[
                pl.ds(pl.multiple_of(group * block + row, SUBLANES), SUBLANES),
                pl.ds(2 * inner + column, length),
            ]
            near = vmem.at[
                pl.ds(pl.multiple_of(group * deep + to_row, SUBLANES), SUBLANES),
                pl.ds(to_column, length),
            ]
            pltpu.make_async_copy(*((far, near) if sides == 0 else (near, far)), sem).start()

    for side in range(2):
        load(0, side).start()

    def fetch_down(group, carry):
        tile_copies(group, 0, feed_ref, down, down_sem)
        return carry

    lax.fori_loop(0, inner // deep, fetch_down, 0)
    for step in range(1, steps):
        for side in range(2):
            load(step, side).start()
    normed, grad = normed_ref[...], grad_ref[...]
    total = resid_ref[...]
    grad_normed = jnp.zeros_like(total)
    for step in range(steps):
        at, next_at = slice(step * chunk, (step + 1) * chunk), slice(
            inner + step * chunk, inner + (step + 1) * chunk
        )
        for side in range(2):
            load(step, side).wait()
        gate = matmul(normed, weights[:, at])
        linear = matmul(normed, weights[:, next_at])
        square = gate * gate
        bend = jnp.tanh(0.7978845608 * gate * (1.0 + 0.044715 * square))
        half = 0.5 * (1.0 + bend)
        value = gate * half
        slope = half + 0.5 * gate * (1.0 - bend * bend) * (
            0.7978845608 * (1.0 + 3.0 * 0.044715 * square)
        )
        hidden = (value * linear).astype(BF)
        if step == 0:
            pltpu.make_async_copy(down, down, down_sem).wait()
        total = total + matmul(hidden, down[at, :])
        grad_hidden = matmul_nt(grad, down[at, :])
        grad_gate = (grad_hidden * linear * slope).astype(BF)
        grad_linear = (grad_hidden * value).astype(BF)
        grad_normed = grad_normed + (
            matmul_nt(grad_gate, weights[:, at]) + matmul_nt(grad_linear, weights[:, next_at])
        )
        terms[:, at] = matmul_tn(normed, grad_gate).astype(BF)
        save(step, 0).start()
        terms[:, next_at] = matmul_tn(normed, grad_linear).astype(BF)
        save(step, 1).start()
        terms_down[at, :] = matmul_tn(hidden, grad).astype(BF)

    def store_down(group, carry):
        tile_copies(group, 1, terms_ref, terms_down, down_out_sem)
        return carry

    lax.fori_loop(0, inner // deep, store_down, 0)
    out_ref[...] = total.astype(BF)
    part, grad_gain = norm_backward(resid_ref[...], gains_ref[2:3, :], grad_normed)
    grad_resid_ref[...] = grad.astype(F32) + part
    grad_gain_ref[...] = grad_gain
    for step in range(steps):
        for side in range(2):
            save(step, side).wait()
    pltpu.make_async_copy(terms_down, terms_down, down_out_sem).wait()


def cross_backward(per_head, grad_ref, resid_ref, normed_ref, rows_ref, kv_ref, mixed_ref,
                   weights_ref, enc_ref, wa_ref, wb_ref, gains_ref,
                   out_ref, grad_gain_ref, terms_a_ref, terms_b_ref, enc_grad_ref,
                   mix_grad, row_grad, kv_grad):
    rows, width = grad_ref.shape
    low = grad_ref[...].astype(BF)
    mix_grad[...] = matmul_nt(low, wb_ref[:, width:]).astype(BF)
    terms_b_ref[:, width:] = matmul_tn(mixed_ref[...], low).astype(BF)
    for pair in range(width // (2 * per_head)):
        at = pl.ds(pair * 2 * per_head, 2 * per_head)
        value_at = pl.ds(width + pair * 2 * per_head, 2 * per_head)
        row_grad[:, at], kv_grad[:, at], kv_grad[:, value_at], _ = attention_pair_grad(
            rows_ref[:, at], kv_ref[:, at], kv_ref[:, value_at], mixed_ref[:, at], mix_grad[:, at],
            weights_ref[pl.ds(pair * 2 * rows, 2 * rows), :], per_head,
        )
    part, grad_gain = norm_backward(
        resid_ref[...], gains_ref[1:2, :], matmul_nt(row_grad[...], wb_ref[:, :width])
    )
    out_ref[...] = grad_ref[...] + part
    grad_gain_ref[...] = grad_gain
    terms_b_ref[:, :width] = matmul_tn(normed_ref[...], row_grad[...]).astype(BF)
    terms_a_ref[...] = matmul_tn(enc_ref[...], kv_grad[...]).astype(BF)
    enc_grad_ref[...] = matmul_nt(kv_grad[...], wa_ref[...])[: enc_grad_ref.shape[0]]


def self_backward(per_head, grad_ref, x_ref, normed_ref, qkv_ref, mixed_ref, weights_ref,
                  wa_ref, wb_ref, gains_ref,
                  out_ref, grad_gain_ref, terms_a_ref, terms_b_ref, score_ref,
                  mix_grad, qkv_grad):
    rows, width = grad_ref.shape
    low = grad_ref[...].astype(BF)
    mix_grad[...] = matmul_nt(low, wb_ref[:, width:]).astype(BF)
    terms_b_ref[:, width:] = matmul_tn(mixed_ref[...], low).astype(BF)
    for pair in range(width // (2 * per_head)):
        at = pl.ds(pair * 2 * per_head, 2 * per_head)
        key_at = pl.ds(width + pair * 2 * per_head, 2 * per_head)
        value_at = pl.ds(2 * width + pair * 2 * per_head, 2 * per_head)
        here = pl.ds(pair * 2 * rows, 2 * rows)
        qkv_grad[:, at], qkv_grad[:, key_at], qkv_grad[:, value_at], grad_scores = (
            attention_pair_grad(
                qkv_ref[:, at], qkv_ref[:, key_at], qkv_ref[:, value_at], mixed_ref[:, at],
                mix_grad[:, at], weights_ref[here, :], per_head,
            )
        )
        for side in range(2):
            score_ref[pl.ds(2 * pair + side, 1), :] = diagonal_sums(
                grad_scores[side * rows : (side + 1) * rows]
            )
    grad_qk, grad_v = qkv_grad[:, : 2 * width], qkv_grad[:, 2 * width :]
    terms_a_ref[...] = matmul_tn(normed_ref[...], grad_qk).astype(BF)
    terms_b_ref[:, :width] = matmul_tn(normed_ref[...], grad_v).astype(BF)
    cotangent = matmul_nt(grad_qk, wa_ref[:, : 2 * width]) + matmul_nt(grad_v, wb_ref[:, :width])
    part, grad_gain = norm_backward(x_ref[...].astype(F32), gains_ref[0:1, :], cotangent)
    out_ref[...] = grad_ref[...] + part
    grad_gain_ref[...] = grad_gain


def whole(kernel, outs, scratch=()):
    return pl.pallas_call(
        kernel,
        out_shape=[jax.ShapeDtypeStruct(*out) for out in outs],
        scratch_shapes=[pltpu.VMEM(*piece) for piece in scratch],
        compiler_params=pltpu.CompilerParams(vmem_limit_bytes=56 << 20),
    )


def body(
    layer_input, encoder_states, output_grad,
    self_query, self_key, self_value, self_output,
    cross_query, cross_key, cross_value, cross_output,
    feed_gate, feed_up, feed_down,
    gain_self, gain_cross, gain_feed,
    bias_table, target_lengths, source_lengths, distance_bucket, *, count,
):
    width = layer_input.shape[1]
    rows = gain_self.shape[0]
    inner = feed_gate.shape[1]
    block = tile_block(width, inner)
    direct = rows % block == 0
    down_piece = to_tiles(feed_down, block, inner) if direct else feed_down.reshape(rows, -1)
    feed_piece = jnp.concatenate([feed_gate, feed_up, down_piece], axis=1)
    feed_all = lax.all_gather(feed_piece, AXIS, axis=0, tiled=True)
    gains = jnp.stack([gain_self, gain_cross, gain_feed], axis=1)
    gains = jnp.pad(gains, ((0, 0), (0, 128 - gains.shape[1])))
    self_piece = jnp.concatenate([self_query, self_key, gains, self_value, self_output], axis=1)
    cross_piece = jnp.concatenate([cross_key, cross_value, cross_query, cross_output], axis=1)
    self_held = gather_high(self_piece, count)
    self_held, cross_piece = tied(self_held, cross_piece)
    self_a, self_b = gather_last(gather_middle(self_held, 2 * width + 128, count), count)
    cross_halves = gather_middle(gather_high(cross_piece, count), 2 * width, count)
    if not direct:
        down_all = feed_all[:, 2 * inner :].reshape(inner, width)
        feed_all = jnp.concatenate(
            [feed_all[:, : 2 * inner], to_tiles(down_all, block, inner)], axis=1
        )

    row_count = layer_input.shape[0]
    onehot = (
        distance_bucket[:, None] == jnp.arange(bias_table.shape[0], dtype=jnp.int32)[None, :]
    ).astype(F32)
    per_distance = jnp.dot(onehot, bias_table, precision=lax.Precision.HIGHEST)
    bias_rows = jnp.pad(per_distance.T, ((0, 0), (0, row_count - per_distance.shape[0])))
    bias = jax.vmap(toeplitz)(bias_rows)
    target_segment = segment_ids(target_lengths[0], row_count)
    source_count = encoder_states.shape[0]
    source_segment = segment_ids(source_lengths[0], source_count)
    position = jnp.arange(row_count, dtype=jnp.int32)
    causal = (target_segment[:, None] == target_segment[None, :]) & (
        position[None, :] <= position[:, None]
    )
    aligned = target_segment[:, None] == source_segment[None, :]
    masked_bias = jnp.where(causal[None], bias, MASKED).reshape(-1, row_count)
    mask = jnp.pad(
        jnp.where(aligned, 0.0, MASKED), ((0, 0), (0, row_count - source_count)),
        constant_values=MASKED,
    )
    encoder = jnp.pad(encoder_states, ((0, row_count - source_count), (0, 0)))
    per_head = width // H
    low, wide = ((row_count, width), BF), ((row_count, width), F32)
    kept = ((H * row_count, row_count), F32)
    one_row = ((1, width), F32)

    gains, normed_one, qkv, mixed_one, weights_one, resid_one = whole(
        partial(self_forward, per_head),
        (((8, width), F32), low, ((row_count, 3 * width), BF), low, kept, wide),
    )(layer_input, self_a, self_b, masked_bias)
    resid_one, *cross_halves = tied(resid_one, *cross_halves)
    cross_a, cross_b = gather_last(cross_halves, count)
    normed_two, cross_rows, cross_kv, mixed_two, weights_two, resid_two, normed_three = whole(
        partial(cross_forward, per_head),
        (low, low, ((row_count, 2 * width), BF), low, kept, wide, low),
    )(resid_one, encoder, cross_a, cross_b, gains, mask)
    chunk = min(512, inner)
    steps = inner // chunk
    in_vmem, in_hbm = pl.BlockSpec(memory_space=pltpu.VMEM), pl.BlockSpec(memory_space=pl.ANY)
    layer_output, grad_resid_two, grad_gain_feed, terms_feed = pl.pallas_call(
        partial(feed_step, chunk, block),
        out_shape=[
            jax.ShapeDtypeStruct(*o) for o in (low, wide, one_row, ((width, 3 * inner), BF))
        ],
        in_specs=[in_vmem] * 4 + [in_hbm],
        out_specs=[in_vmem] * 3 + [in_hbm],
        scratch_shapes=[
            pltpu.VMEM((width, 2 * inner), BF), pltpu.VMEM((inner, width), BF),
            pltpu.VMEM((width, 2 * inner), BF), pltpu.VMEM((inner, width), BF),
            pltpu.SemaphoreType.DMA((steps, 2)), pltpu.SemaphoreType.DMA,
            pltpu.SemaphoreType.DMA((steps, 2)), pltpu.SemaphoreType.DMA,
        ],
        compiler_params=pltpu.CompilerParams(vmem_limit_bytes=56 << 20),
    )(resid_two, normed_three, output_grad, gains, feed_all)
    if not direct:
        terms_down = from_tiles(terms_feed[:, 2 * inner :], block, width)
        terms_feed = jnp.concatenate(
            [terms_feed[:, : 2 * inner], terms_down.reshape(width, inner)], axis=1
        )
    share_feed = lax.psum_scatter(terms_feed, AXIS, scatter_dimension=0, tiled=True).astype(F32)
    share_gate, share_up = share_feed[:, :inner], share_feed[:, inner : 2 * inner]
    share_down = share_feed[:, 2 * inner :]
    share_down = from_tiles(share_down, block, width) if direct else share_down.reshape(feed_down.shape)
    terms = ((width, 2 * width), BF)
    grad_resid_one, grad_gain_cross, terms_ckv, terms_cqo, encoder_grad = whole(
        partial(cross_backward, per_head),
        (wide, one_row, terms, terms, ((source_count, width), F32)),
        (low, low, ((row_count, 2 * width), BF)),
    )(
        grad_resid_two, resid_one, normed_two, cross_rows, cross_kv, mixed_two, weights_two,
        encoder, cross_a, cross_b, gains,
    )
    cross_sum = Reduction(terms_ckv, terms_cqo, count)
    cross_sum.advance()
    (grad_resid_one,) = cross_sum.tie(grad_resid_one)
    cross_sum.advance()
    input_grad, grad_gain_self, terms_qk, terms_vo, grad_scores = whole(
        partial(self_backward, per_head),
        (wide, one_row, terms, terms, ((H, row_count), F32)),
        (low, ((row_count, 3 * width), BF)),
    )(
        grad_resid_one, layer_input, normed_one, qkv, mixed_one, weights_one,
        self_a, self_b, gains,
    )
    self_sum = Reduction(terms_qk, terms_vo, count)
    self_sum.parts[0], self_sum.parts[1] = cross_sum.tie(*self_sum.parts)
    self_sum.advance()
    share_cross = cross_sum.finish()
    grad_bias_rows = jnp.roll(grad_scores[:, ::-1], 1, axis=1)
    grad_table = jnp.dot(
        onehot.T, grad_bias_rows[:, : onehot.shape[0]].T, precision=lax.Precision.HIGHEST
    )
    table_rows = jnp.pad(grad_table, ((0, 0), (0, width - grad_table.shape[1])))
    small = jnp.concatenate(
        [grad_gain_self, grad_gain_cross, grad_gain_feed, table_rows], axis=0
    )
    small = total_sum(small, count)
    share_self = self_sum.finish()
    own = lax.dynamic_slice_in_dim(small[:3], lax.axis_index(AXIS) * rows, rows, axis=1)
    return (
        layer_output, input_grad, encoder_grad,
        *(share_self[:, i * width : (i + 1) * width] for i in range(4)),
        *(share_cross[:, i * width : (i + 1) * width] for i in (2, 0, 1, 3)),
        share_gate, share_up, share_down,
        own[0], own[1], own[2], small[3:, : grad_table.shape[1]],
    )


def solution(mesh):
    count = mesh.shape[AXIS]
    rows, flat, full = P(AXIS, None), P(AXIS), P()

    def step(*args):
        return body(*args, count=count)

    return jax.shard_map(
        step,
        mesh=mesh,
        in_specs=(rows,) * 14 + (flat,) * 3 + (full, rows, rows, full),
        out_specs=(rows,) * 14 + (flat,) * 3 + (full,),
        check_vma=False,
    )
```

```python
from functools import partial

import jax
import jax.numpy as jnp
from jax import lax
from jax.experimental import pallas as pl
from jax.experimental.pallas import tpu as pltpu
from jax.sharding import PartitionSpec as P

H = 12
AXIS = "dp"
EPSILON = 1e-06
MASKED = -1e30
BF = jnp.bfloat16
F32 = jnp.float32


def matmul(left, right):
    return jnp.dot(left, right, preferred_element_type=F32)


def matmul_nt(left, right):
    return lax.dot_general(left, right, (((1,), (1,)), ((), ())), preferred_element_type=F32)


def matmul_tn(left, right):
    return lax.dot_general(left, right, (((0,), (0,)), ((), ())), preferred_element_type=F32)


def partner(count, bit):
    return [(i, i ^ (1 << bit)) for i in range(count)]


def own_bit(bit):
    return (lax.axis_index(AXIS) >> bit) & 1


def tied(*values):
    return lax.optimization_barrier(values)


def split_bits(count):
    bits = count.bit_length() - 1
    assert 1 << bits == count and bits > 2
    return list(range(bits - 1, 2, -1)), (2, 1), 0


def swap_blocks(held, done, bit, count):
    other = lax.ppermute(held, AXIS, partner(count, bit))
    rows, columns = held.shape[1:]
    low = 1 << sum(1 for b in done if b < bit)
    shape = (held.shape[0] // low, 1, low, rows, columns)
    mine, theirs = held.reshape(shape), other.reshape(shape)
    full = (shape[0], 2, *shape[2:])
    ours = lax.broadcasted_iota(jnp.int32, full, 1) == own_bit(bit)
    return jnp.where(
        ours, jnp.broadcast_to(mine, full), jnp.broadcast_to(theirs, full)
    ).reshape(-1, rows, columns)


def gather_high(piece, count):
    high, _, _ = split_bits(count)
    held, done = piece[None], []
    for bit in high:
        held = swap_blocks(held, done, bit, count)
        done.append(bit)
    return held


def gather_middle(held, cut, count, stop=2):
    high, (left, right), _ = split_bits(count)
    halves = []
    for part, pair in ((held[:, :, :cut], (left, right)), (held[:, :, cut:], (right, left))):
        done = list(high)
        for bit in pair[:stop]:
            part = swap_blocks(part, done, bit, count)
            done.append(bit)
        halves.append(part)
    return halves


def gather_second(halves, count):
    high, (left, right), _ = split_bits(count)
    return [
        swap_blocks(halves[0], [*high, left], right, count),
        swap_blocks(halves[1], [*high, right], left, count),
    ]


def gather_last(halves, count):
    high, middle, lowest = split_bits(count)
    done = [*high, *middle]
    return [swap_blocks(p, done, lowest, count).reshape(-1, p.shape[2]) for p in halves]


def fold(held, left, bit, count, last=False):
    rows, columns = held.shape[1:]
    low = 1 << sum(1 for b in left if b < bit)
    view = held.reshape(held.shape[0] // (2 * low), 2, low, rows, columns)
    mine = own_bit(bit)
    sent = lax.dynamic_index_in_dim(view, 1 - mine, 1, keepdims=False)
    kept = lax.dynamic_index_in_dim(view, mine, 1, keepdims=False)
    got = lax.ppermute(sent, AXIS, partner(count, bit))
    total = kept.astype(F32) + got.astype(F32)
    return (total if last else total.astype(BF)).reshape(-1, rows, columns)


class Reduction:
    def __init__(self, first, second, count):
        rows = first.shape[0] // count
        self.count, self.step = count, 0
        self.parts = [t.reshape(count, rows, t.shape[1]) for t in (first, second)]
        high, (one, two), lowest = split_bits(count)
        self.high = high[::-1]
        self.orders = ((lowest, one, two), (lowest, two, one))
        self.left = [list(range(count.bit_length() - 1)) for _ in range(2)]

    def advance(self):
        if self.step < 3:
            for side in range(2):
                bit = self.orders[side][self.step]
                self.parts[side] = fold(self.parts[side], self.left[side], bit, self.count)
                self.left[side].remove(bit)
        else:
            if self.step == 3:
                self.parts = [jnp.concatenate(self.parts, axis=2)]
            bit = self.high[self.step - 3]
            last = self.step - 2 == len(self.high)
            self.parts = [fold(self.parts[0], self.left[0], bit, self.count, last)]
            self.left[0].remove(bit)
        self.step += 1

    def tie(self, *values):
        out = tied(*self.parts, *values)
        self.parts = list(out[: len(self.parts)])
        return out[len(self.parts) :]


def tie_all(groups, value):
    out = list(tied(value, *(part for group in groups for part in group.parts)))
    value = out.pop(0)
    for group in groups:
        group.parts, out = out[: len(group.parts)], out[len(group.parts) :]
    return value


def norm_scale_of(hidden):
    return lax.rsqrt(jnp.mean(hidden * hidden, axis=-1, keepdims=True) + EPSILON)


def norm_backward(hidden, gain, cotangent):
    scale = norm_scale_of(hidden)
    weighted = gain * cotangent
    grad_gain = jnp.sum(cotangent * hidden * scale, axis=0, keepdims=True)
    inner = jnp.mean(weighted * hidden, axis=-1, keepdims=True)
    return scale * weighted - hidden * (scale * scale * scale) * inner, grad_gain


def toeplitz(vector):
    length = vector.shape[0]
    padded = jnp.concatenate([vector[::-1], jnp.zeros((length,), vector.dtype)])
    flattened = jnp.tile(padded, length + 1)[length - 1 : length - 1 + length * (2 * length - 1)]
    return flattened.reshape(length, 2 * length - 1)[:, :length]


def segment_ids(lengths, row_total):
    boundary = jnp.cumsum(lengths)
    row_index = jnp.arange(row_total, dtype=jnp.int32)
    return jnp.sum((row_index[:, None] >= boundary[None, :]).astype(jnp.int32), axis=1)


LANES = 128


def pair_stack(block, per_head):
    first = lax.broadcasted_iota(jnp.int32, block.shape, 1) < per_head
    zero = jnp.zeros_like(block)
    return jnp.concatenate([jnp.where(first, block, zero), jnp.where(first, zero, block)], axis=0)


def side_by_side(stacked):
    rows = stacked.shape[0] // 2
    return jnp.concatenate([stacked[:rows], stacked[rows:]], axis=1)


def attention_pair(query, key, value, bias, per_head):
    scores = matmul_nt(pair_stack(query, per_head), key) + bias
    highest = jnp.max(scores, axis=1, keepdims=True)
    total = jnp.sum(jnp.exp(scores - highest), axis=1, keepdims=True)
    weights = jnp.exp(scores - (highest + jnp.log(total)))
    mixed = matmul(side_by_side(weights.astype(BF)), pair_stack(value, per_head)).astype(BF)
    return mixed, weights


def attention_pair_grad(query, key, value, mixed, grad, weights, per_head):
    product = grad.astype(F32) * mixed.astype(F32)
    first = lax.broadcasted_iota(jnp.int32, product.shape, 1) < per_head
    row_dot = jnp.concatenate(
        [
            jnp.sum(jnp.where(first, product, 0.0), axis=1, keepdims=True),
            jnp.sum(jnp.where(first, 0.0, product), axis=1, keepdims=True),
        ],
        axis=0,
    )
    grad_stack = pair_stack(grad, per_head)
    grad_scores = weights * (matmul_nt(grad_stack, value) - row_dot)
    low = grad_scores.astype(BF)
    grad_query = matmul(side_by_side(low), pair_stack(key, per_head)).astype(BF)
    grad_key = matmul_tn(low, pair_stack(query, per_head)).astype(BF)
    grad_value = matmul_tn(weights.astype(BF), grad_stack).astype(BF)
    return grad_query, grad_key, grad_value, grad_scores


SUBLANES = 8


def tile_block(width, inner):
    block = SUBLANES
    while block * inner % (width * SUBLANES):
        block += SUBLANES
    return block


def to_tiles(array, block, inner):
    width = array.shape[1]
    deep = block * inner // width
    tiles = array.reshape(-1, deep // SUBLANES, SUBLANES, width // LANES, LANES)
    tiles = tiles.transpose(0, 1, 3, 2, 4)
    tiles = tiles.reshape(-1, block // SUBLANES, inner // LANES, SUBLANES, LANES)
    return tiles.transpose(0, 1, 3, 2, 4).reshape(-1, inner)


def from_tiles(array, block, width):
    inner = array.shape[1]
    deep = block * inner // width
    tiles = array.reshape(-1, block // SUBLANES, SUBLANES, inner // LANES, LANES)
    tiles = tiles.transpose(0, 1, 3, 2, 4)
    tiles = tiles.reshape(-1, deep // SUBLANES, width // LANES, SUBLANES, LANES)
    return tiles.transpose(0, 1, 3, 2, 4).reshape(-1, width)


def tile_runs(block, width, inner):
    runs, wide, deep = [], width // LANES, inner // LANES
    for tile in range(block // SUBLANES * deep):
        here = (tile // deep, tile // wide)
        if runs and runs[-1][0] == here:
            runs[-1][3] += LANES
        else:
            runs.append([here, tile % deep * LANES, tile % wide * LANES, LANES])
    return [(h[0] * SUBLANES, c, h[1] * SUBLANES, d, n) for h, c, d, n in runs]


def diagonal_sums(block):
    rows, columns = block.shape
    while rows > 1:
        rows //= 2
        block = block[:rows] + pltpu.roll(block[rows:], (columns - rows) % columns, 1)
    return block


def gain_rows_of(columns):
    return columns.astype(F32).T


def self_forward(per_head, x_ref, wa_ref, wb_ref, bias_ref,
                 gains_ref, normed_ref, qkv_ref, mixed_ref, weights_ref, resid_ref):
    width = x_ref.shape[1]
    rows = x_ref.shape[0]
    gains = gain_rows_of(wa_ref[:, 2 * width :])[:8]
    gains_ref[...] = gains
    resid = x_ref[...].astype(F32)
    normed = (resid * norm_scale_of(resid) * gains[0:1]).astype(BF)
    normed_ref[...] = normed
    qkv_ref[:, : 2 * width] = matmul(normed, wa_ref[:, : 2 * width]).astype(BF)
    qkv_ref[:, 2 * width :] = matmul(normed, wb_ref[:, :width]).astype(BF)
    for pair in range(width // (2 * per_head)):
        at = pl.ds(pair * 2 * per_head, 2 * per_head)
        key_at = pl.ds(width + pair * 2 * per_head, 2 * per_head)
        value_at = pl.ds(2 * width + pair * 2 * per_head, 2 * per_head)
        mixed, weights = attention_pair(
            qkv_ref[:, at], qkv_ref[:, key_at], qkv_ref[:, value_at],
            bias_ref[pl.ds(pair * 2 * rows, 2 * rows), :], per_head,
        )
        mixed_ref[:, at] = mixed
        weights_ref[pl.ds(pair * 2 * rows, 2 * rows), :] = weights
    resid_ref[...] = resid + matmul(mixed_ref[...], wb_ref[:, width:])


def cross_forward(per_head, resid_ref, enc_ref, wa_ref, wb_ref, gains_ref, mask_ref,
                  normed_ref, rows_ref, kv_ref, mixed_ref, weights_ref, out_ref, next_ref):
    rows, width = resid_ref.shape
    resid = resid_ref[...]
    normed = (resid * norm_scale_of(resid) * gains_ref[1:2, :]).astype(BF)
    normed_ref[...] = normed
    rows_ref[...] = matmul(normed, wb_ref[:, :width]).astype(BF)
    kv_ref[...] = matmul(enc_ref[...], wa_ref[...]).astype(BF)
    mask = jnp.concatenate([mask_ref[...], mask_ref[...]], axis=0)
    for pair in range(width // (2 * per_head)):
        at = pl.ds(pair * 2 * per_head, 2 * per_head)
        value_at = pl.ds(width + pair * 2 * per_head, 2 * per_head)
        mixed, weights = attention_pair(
            rows_ref[:, at], kv_ref[:, at], kv_ref[:, value_at], mask, per_head
        )
        mixed_ref[:, at] = mixed
        weights_ref[pl.ds(pair * 2 * rows, 2 * rows), :] = weights
    resid = resid + matmul(mixed_ref[...], wb_ref[:, width:])
    out_ref[...] = resid
    next_ref[...] = (resid * norm_scale_of(resid) * gains_ref[2:3, :]).astype(BF)


def feed_step(chunk, block, resid_ref, normed_ref, grad_ref, gains_ref, feed_ref,
              out_ref, grad_resid_ref, grad_gain_ref, gate_terms_ref, up_terms_ref, down_terms_ref,
              weights, down, terms, terms_down, in_sem, down_sem, out_sem):
    width = resid_ref.shape[1]
    inner = down.shape[0]
    steps = inner // chunk
    deep = block * inner // width
    runs = tile_runs(block, width, inner)

    def columns(step, side):
        return pl.ds(side * inner + step * chunk, chunk)

    def load(step, side):
        at = columns(step, side)
        return pltpu.make_async_copy(feed_ref.at[:, at], weights.at[:, at], in_sem.at[step, side])

    def save(step, side):
        here = pl.ds(step * chunk, chunk)
        if side == 2:
            near, far = terms_down.at[here, :], down_terms_ref.at[here, :]
        else:
            near = terms.at[:, columns(step, side)]
            far = (gate_terms_ref, up_terms_ref)[side].at[:, here]
        return pltpu.make_async_copy(near, far, out_sem.at[step, side])

    for side in range(2):
        load(0, side).start()

    def fetch_down(group, carry):
        for row, column, to_row, to_column, length in runs:
            far = feed_ref.at[
                pl.ds(pl.multiple_of(group * block + row, SUBLANES), SUBLANES),
                pl.ds(2 * inner + column, length),
            ]
            near = down.at[
                pl.ds(pl.multiple_of(group * deep + to_row, SUBLANES), SUBLANES),
                pl.ds(to_column, length),
            ]
            pltpu.make_async_copy(far, near, down_sem).start()
        return carry

    lax.fori_loop(0, inner // deep, fetch_down, 0)
    for step in range(1, steps):
        for side in range(2):
            load(step, side).start()
    normed, grad = normed_ref[...], grad_ref[...]
    total = resid_ref[...]
    grad_normed = jnp.zeros_like(total)
    for step in range(steps):
        at, next_at = slice(step * chunk, (step + 1) * chunk), slice(
            inner + step * chunk, inner + (step + 1) * chunk
        )
        for side in range(2):
            load(step, side).wait()
        gate = matmul(normed, weights[:, at])
        linear = matmul(normed, weights[:, next_at])
        square = gate * gate
        bend = jnp.tanh(0.7978845608 * gate * (1.0 + 0.044715 * square))
        half = 0.5 * (1.0 + bend)
        value = gate * half
        slope = half + 0.5 * gate * (1.0 - bend * bend) * (
            0.7978845608 * (1.0 + 3.0 * 0.044715 * square)
        )
        hidden = (value * linear).astype(BF)
        if step == 0:
            pltpu.make_async_copy(down, down, down_sem).wait()
        total = total + matmul(hidden, down[at, :])
        grad_hidden = matmul_nt(grad, down[at, :])
        grad_gate = (grad_hidden * linear * slope).astype(BF)
        grad_linear = (grad_hidden * value).astype(BF)
        grad_normed = grad_normed + (
            matmul_nt(grad_gate, weights[:, at]) + matmul_nt(grad_linear, weights[:, next_at])
        )
        terms[:, at] = matmul_tn(normed, grad_gate).astype(BF)
        save(step, 0).start()
        terms[:, next_at] = matmul_tn(normed, grad_linear).astype(BF)
        save(step, 1).start()
        terms_down[at, :] = matmul_tn(hidden, grad).astype(BF)
        save(step, 2).start()
    out_ref[...] = total.astype(BF)
    part, grad_gain = norm_backward(resid_ref[...], gains_ref[2:3, :], grad_normed)
    grad_resid_ref[...] = grad.astype(F32) + part
    grad_gain_ref[...] = grad_gain
    for step in range(steps):
        for side in range(3):
            save(step, side).wait()


def cross_backward(per_head, grad_ref, resid_ref, normed_ref, rows_ref, kv_ref, mixed_ref,
                   weights_ref, enc_ref, wa_ref, wb_ref, gains_ref,
                   out_ref, grad_gain_ref, terms_a_ref, terms_b_ref, enc_grad_ref,
                   mix_grad, row_grad, kv_grad):
    rows, width = grad_ref.shape
    low = grad_ref[...].astype(BF)
    mix_grad[...] = matmul_nt(low, wb_ref[:, width:]).astype(BF)
    terms_b_ref[:, width:] = matmul_tn(mixed_ref[...], low).astype(BF)
    for pair in range(width // (2 * per_head)):
        at = pl.ds(pair * 2 * per_head, 2 * per_head)
        value_at = pl.ds(width + pair * 2 * per_head, 2 * per_head)
        row_grad[:, at], kv_grad[:, at], kv_grad[:, value_at], _ = attention_pair_grad(
            rows_ref[:, at], kv_ref[:, at], kv_ref[:, value_at], mixed_ref[:, at], mix_grad[:, at],
            weights_ref[pl.ds(pair * 2 * rows, 2 * rows), :], per_head,
        )
    part, grad_gain = norm_backward(
        resid_ref[...], gains_ref[1:2, :], matmul_nt(row_grad[...], wb_ref[:, :width])
    )
    out_ref[...] = grad_ref[...] + part
    grad_gain_ref[...] = grad_gain
    terms_b_ref[:, :width] = matmul_tn(normed_ref[...], row_grad[...]).astype(BF)
    terms_a_ref[...] = matmul_tn(enc_ref[...], kv_grad[...]).astype(BF)
    enc_grad_ref[...] = matmul_nt(kv_grad[...], wa_ref[...])[: enc_grad_ref.shape[0]]


def self_backward(per_head, grad_ref, x_ref, normed_ref, qkv_ref, mixed_ref, weights_ref,
                  wa_ref, wb_ref, gains_ref,
                  out_ref, grad_gain_ref, terms_a_ref, terms_b_ref, score_ref,
                  mix_grad, qkv_grad):
    rows, width = grad_ref.shape
    low = grad_ref[...].astype(BF)
    mix_grad[...] = matmul_nt(low, wb_ref[:, width:]).astype(BF)
    terms_b_ref[:, width:] = matmul_tn(mixed_ref[...], low).astype(BF)
    for pair in range(width // (2 * per_head)):
        at = pl.ds(pair * 2 * per_head, 2 * per_head)
        key_at = pl.ds(width + pair * 2 * per_head, 2 * per_head)
        value_at = pl.ds(2 * width + pair * 2 * per_head, 2 * per_head)
        here = pl.ds(pair * 2 * rows, 2 * rows)
        qkv_grad[:, at], qkv_grad[:, key_at], qkv_grad[:, value_at], grad_scores = (
            attention_pair_grad(
                qkv_ref[:, at], qkv_ref[:, key_at], qkv_ref[:, value_at], mixed_ref[:, at],
                mix_grad[:, at], weights_ref[here, :], per_head,
            )
        )
        for side in range(2):
            score_ref[pl.ds(2 * pair + side, 1), :] = diagonal_sums(
                grad_scores[side * rows : (side + 1) * rows]
            )
    grad_qk, grad_v = qkv_grad[:, : 2 * width], qkv_grad[:, 2 * width :]
    terms_a_ref[...] = matmul_tn(normed_ref[...], grad_qk).astype(BF)
    terms_b_ref[:, :width] = matmul_tn(normed_ref[...], grad_v).astype(BF)
    cotangent = matmul_nt(grad_qk, wa_ref[:, : 2 * width]) + matmul_nt(grad_v, wb_ref[:, :width])
    part, grad_gain = norm_backward(x_ref[...].astype(F32), gains_ref[0:1, :], cotangent)
    out_ref[...] = grad_ref[...] + part
    grad_gain_ref[...] = grad_gain


def whole(kernel, outs, scratch=()):
    return pl.pallas_call(
        kernel,
        out_shape=[jax.ShapeDtypeStruct(*out) for out in outs],
        scratch_shapes=[pltpu.VMEM(*piece) for piece in scratch],
        compiler_params=pltpu.CompilerParams(vmem_limit_bytes=56 << 20),
    )


def body(
    layer_input, encoder_states, output_grad,
    self_query, self_key, self_value, self_output,
    cross_query, cross_key, cross_value, cross_output,
    feed_gate, feed_up, feed_down,
    gain_self, gain_cross, gain_feed,
    bias_table, target_lengths, source_lengths, distance_bucket, *, count,
):
    width = layer_input.shape[1]
    rows = gain_self.shape[0]
    inner = feed_gate.shape[1]
    block = tile_block(width, inner)
    direct = rows % block == 0
    down_piece = to_tiles(feed_down, block, inner) if direct else feed_down.reshape(rows, -1)
    feed_piece = jnp.concatenate([feed_gate, feed_up, down_piece], axis=1)
    feed_all = lax.all_gather(feed_piece, AXIS, axis=0, tiled=True)
    gains = jnp.stack([gain_self, gain_cross, gain_feed], axis=1)
    gains = jnp.pad(gains, ((0, 0), (0, 128 - gains.shape[1])))
    self_piece = jnp.concatenate([self_query, self_key, gains, self_value, self_output], axis=1)
    cross_piece = jnp.concatenate([cross_key, cross_value, cross_query, cross_output], axis=1)
    row_count = layer_input.shape[0]
    onehot = (
        distance_bucket[:, None] == jnp.arange(bias_table.shape[0], dtype=jnp.int32)[None, :]
    ).astype(F32)
    per_distance = jnp.dot(onehot, bias_table, precision=lax.Precision.HIGHEST)
    bias_rows = jnp.pad(per_distance.T, ((0, 0), (0, row_count - per_distance.shape[0])))
    bias = jax.vmap(toeplitz)(bias_rows)
    target_segment = segment_ids(target_lengths[0], row_count)
    source_count = encoder_states.shape[0]
    source_segment = segment_ids(source_lengths[0], source_count)
    position = jnp.arange(row_count, dtype=jnp.int32)
    causal = (target_segment[:, None] == target_segment[None, :]) & (
        position[None, :] <= position[:, None]
    )
    aligned = target_segment[:, None] == source_segment[None, :]
    masked_bias = jnp.where(causal[None], bias, MASKED).reshape(-1, row_count)
    mask = jnp.pad(
        jnp.where(aligned, 0.0, MASKED), ((0, 0), (0, row_count - source_count)),
        constant_values=MASKED,
    )
    encoder = jnp.pad(encoder_states, ((0, row_count - source_count), (0, 0)))
    self_held = gather_high(self_piece, count)
    self_held, cross_piece, masked_bias, mask, encoder = tied(
        self_held, cross_piece, masked_bias, mask, encoder
    )
    self_halves = gather_middle(self_held, 2 * width + 128, count)
    cross_held = gather_high(cross_piece, count)
    *self_halves, cross_held = tied(*self_halves, cross_held)
    self_a, self_b = gather_last(self_halves, count)
    cross_halves = gather_middle(cross_held, 2 * width, count, 1)
    if not direct:
        down_all = feed_all[:, 2 * inner :].reshape(inner, width)
        feed_all = jnp.concatenate(
            [feed_all[:, : 2 * inner], to_tiles(down_all, block, inner)], axis=1
        )

    per_head = width // H
    low, wide = ((row_count, width), BF), ((row_count, width), F32)
    kept = ((H * row_count, row_count), F32)
    one_row = ((1, width), F32)

    gains, normed_one, qkv, mixed_one, weights_one, resid_one = whole(
        partial(self_forward, per_head),
        (((8, width), F32), low, ((row_count, 3 * width), BF), low, kept, wide),
    )(layer_input, self_a, self_b, masked_bias)
    resid_one, *cross_halves = tied(resid_one, *cross_halves)
    cross_a, cross_b = gather_last(gather_second(cross_halves, count), count)
    normed_two, cross_rows, cross_kv, mixed_two, weights_two, resid_two, normed_three = whole(
        partial(cross_forward, per_head),
        (low, low, ((row_count, 2 * width), BF), low, kept, wide, low),
    )(resid_one, encoder, cross_a, cross_b, gains, mask)
    chunk = min(512, inner)
    steps = inner // chunk
    in_vmem, in_hbm = pl.BlockSpec(memory_space=pltpu.VMEM), pl.BlockSpec(memory_space=pl.ANY)
    terms_feed = ((width, inner), BF)
    layer_output, grad_resid_two, grad_gain_feed, terms_gate, terms_up, terms_down = pl.pallas_call(
        partial(feed_step, chunk, block),
        out_shape=[
            jax.ShapeDtypeStruct(*o) for o in (low, wide, one_row, terms_feed, terms_feed, ((inner, width), BF))
        ],
        in_specs=[in_vmem] * 4 + [in_hbm],
        out_specs=[in_vmem] * 3 + [in_hbm] * 3,
        scratch_shapes=[
            pltpu.VMEM((width, 2 * inner), BF), pltpu.VMEM((inner, width), BF),
            pltpu.VMEM((width, 2 * inner), BF), pltpu.VMEM((inner, width), BF),
            pltpu.SemaphoreType.DMA((steps, 2)), pltpu.SemaphoreType.DMA,
            pltpu.SemaphoreType.DMA((steps, 3)),
        ],
        compiler_params=pltpu.CompilerParams(vmem_limit_bytes=56 << 20),
    )(resid_two, normed_three, output_grad, gains, feed_all)
    share_down = lax.psum_scatter(terms_down, AXIS, scatter_dimension=0, tiled=True).astype(F32)
    feed_sum = Reduction(terms_gate, terms_up, count)
    feed_sum.advance()
    terms = ((width, 2 * width), BF)
    grad_resid_one, grad_gain_cross, terms_ckv, terms_cqo, encoder_grad = whole(
        partial(cross_backward, per_head),
        (wide, one_row, terms, terms, ((source_count, width), F32)),
        (low, low, ((row_count, 2 * width), BF)),
    )(
        grad_resid_two, resid_one, normed_two, cross_rows, cross_kv, mixed_two, weights_two,
        encoder, cross_a, cross_b, gains,
    )
    cross_sum = Reduction(terms_ckv, terms_cqo, count)
    grad_resid_one, *cross_sum.parts = feed_sum.tie(grad_resid_one, *cross_sum.parts)
    feed_sum.advance()
    cross_sum.advance()
    input_grad, grad_gain_self, terms_qk, terms_vo, grad_scores = whole(
        partial(self_backward, per_head),
        (wide, one_row, terms, terms, ((H, row_count), F32)),
        (low, ((row_count, 3 * width), BF)),
    )(
        grad_resid_one, layer_input, normed_one, qkv, mixed_one, weights_one,
        self_a, self_b, gains,
    )
    self_sum = Reduction(terms_qk, terms_vo, count)
    grad_bias_rows = jnp.roll(grad_scores[:, ::-1], 1, axis=1)
    grad_table = jnp.dot(
        onehot.T, grad_bias_rows[:, : onehot.shape[0]].T, precision=lax.Precision.HIGHEST
    )
    table_size = grad_table.size
    table_row = jnp.pad(grad_table.reshape(-1), (0, -table_size % width)).reshape(-1, width)
    small = jnp.concatenate([grad_gain_self, grad_gain_cross, grad_gain_feed, table_row], axis=0)
    groups, bit = [feed_sum, cross_sum, self_sum], 0
    small = tie_all(groups, small)
    while any(group.left[0] for group in groups):
        for group in groups:
            if group.left[0]:
                group.advance()
        if 1 << bit < count:
            small = small + lax.ppermute(small, AXIS, partner(count, bit))
            bit += 1
        small = tie_all(groups, small)
    assert 1 << bit == count
    share_feed, share_cross, share_self = (group.parts[0][0] for group in groups)
    share_gate, share_up = share_feed[:, :inner], share_feed[:, inner:]
    own = lax.dynamic_slice_in_dim(small[:3], lax.axis_index(AXIS) * rows, rows, axis=1)
    return (
        layer_output, input_grad, encoder_grad,
        *(share_self[:, i * width : (i + 1) * width] for i in range(4)),
        *(share_cross[:, i * width : (i + 1) * width] for i in (2, 0, 1, 3)),
        share_gate, share_up, share_down,
        own[0], own[1], own[2], small[3:].reshape(-1)[:table_size].reshape(grad_table.shape),
    )


def solution(mesh):
    count = mesh.shape[AXIS]
    rows, flat, full = P(AXIS, None), P(AXIS), P()

    def step(*args):
        return body(*args, count=count)

    return jax.shard_map(
        step,
        mesh=mesh,
        in_specs=(rows,) * 14 + (flat,) * 3 + (full, rows, rows, full),
        out_specs=(rows,) * 14 + (flat,) * 3 + (full,),
        check_vma=False,
    )
```
